32 devices in a mesh: old: 8 (over z, core), new: 4 (over y, x).
Axes of the slice: x: 2, y: 2, z: 4, core: 2. Of those that a mesh axis runs over, the one named last changes fastest.
Arguments:
- centroids_old: bfloat16 [65536, 768], P(('old', 'new')), may hold values from -6 to 6
- centroids_new: bfloat16 [16384, 768], P(('old', 'new')), may hold values from -6 to 6
- mass_old: float32 [65536], P(('old', 'new')), may hold values from 0.5 to 18
- mass_new: float32 [16384], P(('old', 'new')), may hold values from 0.5 to 18
- pairs: int32 [256, 8], P(('old', 'new')), may hold values from 0 to 63, as said below
Outputs:
- log_old: float32 [65536], P(('old', 'new'))
- log_new: float32 [16384], P(('old', 'new'))
The draws below stay inside these ranges and needn't reach their ends.
Inputs may be any that keep to these rules, and one draw needn't show every extreme that they name: `pairs`: each row names 8 different new blocks, all held by devices with the same index along old as the device that holds that old block. The rows held by one device name, of the blocks of each such device, exactly 2 different blocks. Every new block is named by some row.
All inputs are finite; a program needn't handle non-finite values.
Results may differ from the reference program's by a relative error of at most 0.0003.
Values may be sent and summed in bfloat16 or wider, within the bound.
A program may use at most 128 MiB of HBM per device.

```python
import jax
import jax.numpy as jnp
from jax import lax

D = 768
CENTROID_BLOCK = 256
PARTNER_BLOCKS = 8
ITERS = 3
OBD = 8
NBD = 2
GROUPS = 8
OWNERS = 4
CAP = 2
NBO = 256
NBN = 64
NO = 65536
NN = 16384


def draw_mass_old(key, part):
    place = jnp.arange(NO).astype(jnp.float32) / NO
    base = jnp.exp(jax.random.uniform(key, (NO,), jnp.float32, -0.6931, 0.6931))
    ramp = 1.0 + 2.0 * place
    return base * ramp


def draw_mass_new(key, part):
    place = jnp.arange(NN).astype(jnp.float32) / NN
    base = jnp.exp(jax.random.uniform(key, (NN,), jnp.float32, -0.6931, 0.6931))
    ramp = 1.0 + 2.0 * place
    return base * ramp


def draw_pairs(key, part):
    count = GROUPS * OWNERS
    width = OWNERS * CAP
    offsets = jax.random.randint(jax.random.fold_in(key, 1), (count,), 0, NBD)
    first_draw = jax.random.randint(jax.random.fold_in(key, 2), (count, OWNERS), 0, NBD)
    second_draw = jax.random.randint(jax.random.fold_in(key, 3), (count, OWNERS), 0, NBD)
    requester = jnp.arange(count)
    column_pos = requester % OWNERS
    owner_flat = (requester // OWNERS)[:, None] * OWNERS + jnp.arange(OWNERS)[None, :]
    covering = (column_pos * CAP < NBD)[:, None]
    start_block = jnp.where(covering, column_pos[:, None] * CAP, jnp.minimum(first_draw, second_draw)) + offsets[owner_flat]
    block_ids = owner_flat[:, :, None] * NBD + (start_block[:, :, None] + jnp.arange(CAP)[None, None, :]) % NBD
    block_ids = block_ids.reshape(count, width)
    shuffle = jax.vmap(lambda subkey: jax.random.permutation(subkey, width))(jax.random.split(jax.random.fold_in(key, 4), count))
    row_pos = jnp.arange(OBD)
    random_starts = jax.random.randint(jax.random.fold_in(key, 5), (count, OBD), 0, width)
    starts = jnp.where((row_pos * PARTNER_BLOCKS < width)[None, :], (row_pos * PARTNER_BLOCKS)[None, :], random_starts)
    places = (starts[:, :, None] + jnp.arange(PARTNER_BLOCKS)[None, None, :]) % width
    elements = jnp.take_along_axis(shuffle, places.reshape(count, OBD * PARTNER_BLOCKS), axis=1)
    result = jnp.take_along_axis(block_ids, elements, axis=1)
    return result.reshape(count * OBD, PARTNER_BLOCKS).astype(jnp.int32)


def block_scale(stream_key, extent, pieces, smallest, top_value):
    def one(position, shards_of):
        steps = jax.random.uniform(jax.random.fold_in(jax.random.fold_in(stream_key, 6), position), (shards_of,), jnp.float32, smallest / len(pieces), top_value / len(pieces))
        return jnp.repeat(jnp.exp(steps), extent[position] // shards_of).reshape((-1,) + (1,) * (len(extent) - position - 1))

    gain = one(*pieces[0])
    for cut in pieces[1:]:
        gain = gain * one(*cut)
    return gain


def normal_values(own_key, shape, deviation, reach, cuts=(), dtype=jnp.bfloat16):
    array = deviation * jax.random.normal(own_key, shape, jnp.float32)
    if cuts:
        array = array * block_scale(own_key, shape, cuts, -0.22, 0.18)
    return jnp.clip(array, -reach, reach).astype(dtype)


def setup_inputs(seed: int = 0) -> dict:
    keys = jax.random.split(jax.random.key(seed), 6)
    centroids_old = normal_values(keys[0], (NO, D), 1.0, 6.0, ((0, 32),))
    centroids_new = normal_values(keys[1], (NN, D), 1.0, 6.0, ((0, 32),))
    mass_old = draw_mass_old(jax.random.fold_in(keys[5], 71), 0)
    mass_new = draw_mass_new(jax.random.fold_in(keys[5], 71), 0)
    pairs = draw_pairs(jax.random.fold_in(keys[5], 71), 0)
    return {"centroids_old": centroids_old, "centroids_new": centroids_new, "mass_old": mass_old, "mass_new": mass_new, "pairs": pairs}


ENTROPY_SCALE = 0.025

def reference(centroids_old, centroids_new, mass_old, mass_new, pairs):
    old_blocks = centroids_old.reshape(NBO, CENTROID_BLOCK, D)
    new_blocks = centroids_new.reshape(NBN, CENTROID_BLOCK, D)
    previous_norm = jnp.sqrt(lax.optimization_barrier(jnp.sum(jnp.square(old_blocks.astype(jnp.float32)), axis=-1)) + 1e-06)
    norm_new = jnp.sqrt(lax.optimization_barrier(jnp.sum(jnp.square(new_blocks.astype(jnp.float32)), axis=-1)) + 1e-06)

    def build_tiles(inputs_row):
        row_block, row_norm_values, row_ids = inputs_row
        chosen = new_blocks[row_ids]
        inner_products = jnp.einsum('bd,kcd->kbc', row_block.astype(jnp.float32), chosen.astype(jnp.float32), precision=lax.Precision.HIGHEST)
        selected_norm = norm_new[row_ids]
        return jnp.exp(inner_products / (row_norm_values[None, :, None] * selected_norm[:, None, :]) / ENTROPY_SCALE) * (1.0 / (PARTNER_BLOCKS * CENTROID_BLOCK))
    kernel = lax.map(build_tiles, (old_blocks, previous_norm, pairs))
    rel_old = (mass_old * (NO / jnp.sum(mass_old))).reshape(NBO, CENTROID_BLOCK)
    rel_new = (mass_new * (NN / jnp.sum(mass_new))).reshape(NBN, CENTROID_BLOCK)
    scales = jnp.ones((NBN, CENTROID_BLOCK), jnp.float32)
    left_scale = jnp.ones((NBO, CENTROID_BLOCK), jnp.float32)
    for sweep_index in range(ITERS):
        picked = scales[pairs]
        row_sum = jnp.einsum('ikbc,ikc->ib', kernel, picked, precision=lax.Precision.HIGHEST)
        left_scale = rel_old / row_sum
        col_terms = jnp.einsum('ikbc,ib->ikc', kernel, left_scale, precision=lax.Precision.HIGHEST)
        column = jax.ops.segment_sum(col_terms.reshape(-1, CENTROID_BLOCK), pairs.reshape(-1), num_segments=NBN)
        scales = rel_new / column
    return (jnp.log(left_scale).reshape(NO), jnp.log(scales).reshape(NN))
```

```python
import functools
import math

import jax
import jax.numpy as jnp
from jax import lax
from jax.experimental import pallas as pl
from jax.experimental.pallas import tpu as pltpu
from jax.sharding import PartitionSpec as P

D = 768
CENTROID_BLOCK = 256
PARTNER_BLOCKS = 8
ITERS = 3


ENTROPY_SCALE = 0.025


def row_norm_values(blocks):
    return jnp.sqrt(jnp.sum(jnp.square(blocks.astype(jnp.float32)), axis=-1) + 1e-06)


def general_body(centroids_old, centroids_new, mass_old, mass_new, pairs):
    owners = lax.axis_size("new")
    my_old = lax.axis_index("old")
    old_count = centroids_old.shape[0] // CENTROID_BLOCK
    new_count = centroids_new.shape[0] // CENTROID_BLOCK
    devices_all = lax.axis_size("old") * owners
    totals = lax.psum((jnp.sum(mass_old), jnp.sum(mass_new)), ("old", "new"))
    rel_old = (mass_old * (mass_old.shape[0] * devices_all / totals[0])).reshape(
        old_count, CENTROID_BLOCK
    )
    rel_new = (mass_new * (mass_new.shape[0] * devices_all / totals[1])).reshape(
        new_count, CENTROID_BLOCK
    )
    old_blocks = centroids_old.reshape(old_count, CENTROID_BLOCK, D)
    previous_norm = row_norm_values(old_blocks)
    local_ids = pairs - my_old * (owners * new_count)
    everyone = lax.all_gather(centroids_new, "new", axis=0, tiled=True).reshape(
        owners * new_count, CENTROID_BLOCK, D
    )
    norm_all = row_norm_values(everyone)
    chosen = everyone[local_ids]
    selected_norm = norm_all[local_ids]
    columns = owners * new_count
    inner_products = jnp.einsum(
        "rbd,rkcd->rkbc", old_blocks, chosen, preferred_element_type=jnp.float32
    )
    kernel = jnp.exp(
        inner_products
        / (previous_norm[:, None, :, None] * selected_norm[:, :, None, :])
        / ENTROPY_SCALE
    ) * (1.0 / (PARTNER_BLOCKS * CENTROID_BLOCK))
    selector = (local_ids.reshape(-1)[:, None] == jnp.arange(columns)[None, :]).astype(jnp.float32)
    scales = jnp.ones((new_count, CENTROID_BLOCK), jnp.float32)
    left_scale = jnp.ones((old_count, CENTROID_BLOCK), jnp.float32)
    for sweep_index in range(ITERS):
        if sweep_index == 0:
            picked = jnp.ones((old_count, PARTNER_BLOCKS, CENTROID_BLOCK), jnp.float32)
        else:
            fetched = lax.all_gather(scales, "new", axis=0, tiled=True)
            picked = fetched[local_ids]
        row_sum = jnp.einsum("ikbc,ikc->ib", kernel, picked, precision=lax.Precision.HIGHEST)
        left_scale = rel_old / row_sum
        col_terms = jnp.einsum("ikbc,ib->ikc", kernel, left_scale, precision=lax.Precision.HIGHEST)
        gathered_terms = jnp.dot(
            selector.T,
            col_terms.reshape(-1, CENTROID_BLOCK),
            precision=lax.Precision.HIGHEST,
            preferred_element_type=jnp.float32,
        )
        column = lax.psum_scatter(gathered_terms, "new", scatter_dimension=0, tiled=True)
        scales = rel_new / column
    return (jnp.log(left_scale).reshape(-1), jnp.log(scales).reshape(-1))


MESH = pl.DeviceIdType.MESH
LANES = 128
SUBLANES = 8
TILE = 256
STAGE_TILE = 512
UNROLL = 4


def eye_mask():
    shape = (LANES, LANES)
    return lax.broadcasted_iota(jnp.int32, shape, 0) == lax.broadcasted_iota(jnp.int32, shape, 1)


def to_row(column, eye):
    wide = jnp.broadcast_to(column, (LANES, LANES))
    return jnp.sum(jnp.where(eye, wide, 0.0), axis=0, keepdims=True)


def to_column(row, eye):
    wide = jnp.broadcast_to(row, (LANES, LANES))
    return jnp.sum(jnp.where(eye, wide, 0.0), axis=1, keepdims=True)


def dense_kernel(
    olds,
    devices_all,
    old_hbm,
    new_hbm,
    mass_old_hbm,
    mass_new_hbm,
    left_ref,
    scales_ref,
    mass_old_ref,
    mass_new_ref,
    a_ref,
    b_ref,
    k_ref,
    inv_old,
    mass_wide,
    row_acc,
    u_ref,
    col_acc,
    v_ref,
    rel_new,
    meta,
    meta_in,
    sums,
    sums_in,
    cols,
    cols_in,
    load_sem,
    gather_send,
    gather_recv,
    meta_send,
    meta_recv,
    sums_send,
    sums_recv,
    cols_send,
    cols_recv,
):
    me = lax.axis_index("new")
    my_old = lax.axis_index("old")
    flip_x = 1 - 2 * lax.rem(me, 2)
    flip_y = 2 - 4 * lax.div(me, 2)
    peers = (None, me + flip_x, me + flip_y, me + flip_x + flip_y)
    old_steps = olds.bit_length() - 1
    old_peers = [
        my_old + (1 << k) - (2 << k) * lax.rem(lax.div(my_old, 1 << k), 2) for k in range(old_steps)
    ]

    n_old = a_ref.shape[0]
    half = b_ref.shape[2]
    depth = a_ref.shape[1]
    r = mass_new_ref.shape[0]
    tiles = n_old // TILE
    per_tile = TILE // LANES
    per_half = half // LANES
    scale = float(PARTNER_BLOCKS * CENTROID_BLOCK)
    eye = eye_mask()

    load_a = pltpu.make_async_copy(old_hbm, a_ref, load_sem.at[0])
    load_b = [
        pltpu.make_async_copy(new_hbm.at[h], b_ref.at[0, h], load_sem.at[1 + h]) for h in range(2)
    ]
    load_mass = [
        pltpu.make_async_copy(mass_old_hbm, mass_old_ref, load_sem.at[3]),
        pltpu.make_async_copy(mass_new_hbm, mass_new_ref, load_sem.at[4]),
    ]
    barrier = pltpu.get_barrier_semaphore()
    for p in range(1, 4):
        pl.semaphore_signal(barrier, inc=1, device_id={"new": peers[p]}, device_id_type=MESH)
    for peer in old_peers:
        pl.semaphore_signal(barrier, inc=1, device_id={"old": peer}, device_id_type=MESH)
    for copy in load_mass + [load_a] + load_b:
        copy.start()
    pl.semaphore_wait(barrier, 3 + len(old_peers))

    meta_copies = [
        pltpu.make_async_remote_copy(
            src_ref=meta,
            dst_ref=meta_in.at[p - 1],
            send_sem=meta_send.at[p - 1],
            recv_sem=meta_recv.at[p - 1],
            device_id={"new": peers[p]},
            device_id_type=MESH,
        )
        for p in range(1, 4)
    ]

    def send(index, src, slot, h, p, part=None):
        return pltpu.make_async_remote_copy(
            src_ref=src,
            dst_ref=b_ref.at[slot, h] if part is None else b_ref.at[slot, h, part],
            send_sem=gather_send.at[index],
            recv_sem=gather_recv.at[index],
            device_id={"new": peers[p]},
            device_id_type=MESH,
        )

    moves = [
        send(0, new_hbm.at[1], 1, 1, 1),
        send(1, new_hbm.at[0], 1, 0, 1),
        send(2, new_hbm.at[0], 2, 0, 2),
        send(3, new_hbm.at[1], 2, 1, 2),
    ]
    quarters = [pl.ds(q * (half // 2), half // 2) for q in range(2)]
    relay_x = [send(4 + q, b_ref.at[2, 0, quarters[q]], 3, 0, 1, quarters[q]) for q in range(2)]
    relay_y = [send(6 + q, b_ref.at[1, 1, quarters[q]], 3, 1, 2, quarters[q]) for q in range(2)]
    core = lax.rem(my_old, 2)

    def start_moves():
        for index in (0, 2, 1, 3):
            moves[index].start()

    pl.when(core == 0)(start_moves)

    for copy in load_mass:
        copy.wait()
    meta[...] = jnp.zeros_like(meta)
    meta[0:r, :] = mass_new_ref[...]
    meta[r : r + 1, :] = jnp.sum(mass_old_ref[...], axis=0, keepdims=True)
    for copy in meta_copies:
        copy.start()
    load_a.wait()

    @pl.loop(0, tiles)
    def _(t):
        rows = pl.ds(pl.multiple_of(t * TILE, TILE), TILE)
        a = a_ref[rows, :].astype(jnp.float32)
        total = jnp.sum(a * a, axis=1, keepdims=True)
        inv_old[rows, :] = jnp.broadcast_to(1.0 / jnp.sqrt(total + 1e-06), (TILE, LANES))
        for i in range(per_tile):
            part = pl.ds(pl.multiple_of(t * TILE + i * LANES, LANES), LANES)
            column = to_column(mass_old_ref[pl.ds(t * per_tile + i, 1), :], eye)
            mass_wide[part, :] = jnp.broadcast_to(column * scale, (LANES, LANES))

    def stage(chunks, first, start=0, width=None):
        width = half if width is None else width
        factors = []
        for slot, h in chunks:
            b = b_ref[slot, h, start : start + width].astype(jnp.float32)
            total = jnp.sum(b * b, axis=1, keepdims=True)
            inverse = (math.log2(math.e) / ENTROPY_SCALE) / jnp.sqrt(total + 1e-06)
            factors.append(
                [to_row(inverse[j : j + LANES], eye) for j in range(0, width, LANES)]
            )

        @pl.loop(0, n_old // STAGE_TILE)
        def _(t):
            rows = pl.ds(pl.multiple_of(t * STAGE_TILE, STAGE_TILE), STAGE_TILE)
            a = a_ref[rows, :]
            inv = inv_old[rows, :]
            acc = jnp.zeros((STAGE_TILE, LANES), jnp.float32) if first else row_acc[rows, :]
            for some in [chunks] if width < half else [(chunk,) for chunk in chunks]:
                blocks = [b_ref[slot, h, start : start + width] for slot, h in some]
                products = lax.dot_general(
                    a,
                    jnp.concatenate(blocks, axis=0) if len(blocks) > 1 else blocks[0],
                    (((1,), (1,)), ((), ())),
                    preferred_element_type=jnp.float32,
                )
                for i, (slot, h) in enumerate(some):
                    factor = factors[chunks.index((slot, h))]
                    for j in range(0, width, LANES):
                        part = products[:, i * width + j : i * width + j + LANES]
                        k = jnp.exp2(part * inv * factor[j // LANES])
                        k_ref[2 * slot + h, rows, start + j : start + j + LANES] = k
                        acc = acc + k
            row_acc[rows, :] = acc

    for copy in load_b:
        copy.wait()
    sums_copies = [
        pltpu.make_async_remote_copy(
            src_ref=sums.at[k],
            dst_ref=sums_in.at[k],
            send_sem=sums_send.at[k],
            recv_sem=sums_recv.at[k],
            device_id={"old": peer},
            device_id_type=MESH,
        )
        for k, peer in enumerate(old_peers)
    ]

    def advance(k):
        sums_copies[k].wait()
        sums[k + 1] = sums[k] + sums_in[k]
        if k + 1 < old_steps:
            sums_copies[k + 1].start()

    stage(((0, 0), (0, 1)), True)
    pl.when(core == 1)(start_moves)
    moves[0].wait_recv()
    for copy in relay_y:
        copy.start()
    moves[2].wait_recv()
    for copy in relay_x:
        copy.start()
    stage(((1, 1), (2, 0)), False)
    moves[1].wait_recv()
    moves[3].wait_recv()
    stage(((1, 0), (2, 1)), False)
    for copy in meta_copies:
        copy.wait()
    old_sum = meta[r : r + 1, :]
    new_sum = jnp.sum(meta[0:r, :], axis=0, keepdims=True)
    for p in range(1, 4):
        old_sum = old_sum + meta_in[p - 1, r : r + 1, :]
        new_sum = new_sum + jnp.sum(meta_in[p - 1, 0:r, :], axis=0, keepdims=True)
    sums[0] = jnp.zeros((SUBLANES, LANES), jnp.float32)
    sums[0, 0:1, :] = old_sum
    sums[0, 1:2, :] = new_sum
    sums_copies[0].start()
    rel_new[0] = meta[0:r, :] * scale
    for p in range(1, 4):
        rel_new[p] = meta_in[p - 1, 0:r, :] * scale
    for piece in range(2):
        relay_x[piece].wait_recv()
        relay_y[piece].wait_recv()
        stage(((3, 0), (3, 1)), False, piece * (half // 2), half // 2)
    for move in moves + relay_x + relay_y:
        move.wait_send()

    my_x, my_y = lax.rem(me, 2), lax.div(me, 2)

    def slot_of(owner):
        x = 1 - my_x if owner % 2 else my_x
        y = 1 - my_y if owner // 2 else my_y
        return x + 2 * y

    def col_sums(slot):
        @pl.loop(0, tiles // UNROLL, init_carry=[jnp.zeros((SUBLANES, LANES), jnp.float32)] * r)
        def sums_of(t, carry):
            for b in range(UNROLL):
                start = (t * UNROLL + b) * TILE
                rows = pl.ds(pl.multiple_of(start, TILE), TILE)
                u = u_ref[rows, :]
                new = []
                for g in range(r):
                    c, j = 2 * slot + g // per_half, g % per_half
                    part = k_ref[c, rows, j * LANES : (j + 1) * LANES] * u
                    part = part.reshape(TILE // SUBLANES, SUBLANES, LANES)
                    new.append(carry[g] + jnp.sum(part, axis=0))
                carry = new
            return carry

        for g in range(r):
            col_acc[g] = sums_of[g]
        return jnp.sum(col_acc[...], axis=1)

    def add_rows(slot, owner, first):
        @pl.loop(0, tiles // UNROLL)
        def _(t):
            for b in range(UNROLL):
                start = (t * UNROLL + b) * TILE
                rows = pl.ds(pl.multiple_of(start, TILE), TILE)
                acc = jnp.zeros((TILE, LANES), jnp.float32) if first else row_acc[rows, :]
                for g in range(r):
                    c, j = 2 * slot + g // per_half, g % per_half
                    weights = v_ref[owner, g : g + 1, :]
                    acc = acc + k_ref[c, rows, j * LANES : (j + 1) * LANES] * weights
                row_acc[rows, :] = acc

    def exchange(sweep, index, p, src):
        return pltpu.make_async_remote_copy(
            src_ref=cols.at[sweep, src],
            dst_ref=cols_in.at[sweep, p - 1, index],
            send_sem=cols_send.at[sweep, p - 1, index],
            recv_sem=cols_recv.at[sweep, p - 1, index],
            device_id={"new": peers[p]},
            device_id_type=MESH,
        )

    for sweep in range(ITERS):
        last = sweep == ITERS - 1

        @pl.loop(0, n_old // STAGE_TILE)
        def _(t):
            rows = pl.ds(pl.multiple_of(t * STAGE_TILE, STAGE_TILE), STAGE_TILE)
            row_sum = jnp.sum(row_acc[rows, :], axis=1, keepdims=True)
            u_ref[rows, :] = mass_wide[rows, :] / jnp.broadcast_to(row_sum, (STAGE_TILE, LANES))

        if last:
            copies = []
            for p in (3, 2, 1):
                cols[sweep, p] = col_sums(p)
                copies.append(exchange(sweep, 0, p, p))
                copies[-1].start()
            total = col_sums(0)
            for k in range(ITERS - 1, old_steps):
                advance(k)
            totals = jnp.sum(sums[old_steps], axis=1, keepdims=True)
            alpha = n_old * devices_all / totals[0:1, :]
            beta = r * LANES * devices_all / totals[1:2, :]
            ratio = alpha / beta
            left_factor, scales_factor = alpha, 1.0 / ratio
            for _ in range(ITERS - 1):
                left_factor, scales_factor = left_factor * ratio, scales_factor / ratio
            for i in range(n_old // LANES):
                left_ref[i : i + 1, :] = (
                    to_row(u_ref[i * LANES : (i + 1) * LANES, :], eye) * left_factor
                )
            for copy in copies:
                copy.wait()
            for p in range(1, 4):
                total = total + cols_in[sweep, p - 1, 0]
            scales_ref[...] = rel_new[0] / total * scales_factor
        else:
            copies = []
            for owner in range(4):
                cols[sweep, owner] = col_sums(slot_of(owner))
                copies.append([exchange(sweep, owner, p, owner) for p in (3, 2, 1)])
                for copy in copies[-1]:
                    copy.start()
            if sweep < old_steps:
                advance(sweep)
            for owner in range(4):
                for copy in copies[owner]:
                    copy.wait()
                slot = slot_of(owner)
                total = cols[sweep, owner]
                for p in range(1, 4):
                    total = total + cols_in[sweep, p - 1, owner]
                v_ref[owner] = rel_new[slot] / total
                add_rows(slot, owner, owner == 0)


def log_kernel(left_ref, scales_ref, log_old_ref, log_new_ref):
    log_old_ref[...] = jnp.log(left_ref[...])
    log_new_ref[...] = jnp.log(scales_ref[...])


def dense_body(mesh, centroids_old, centroids_new, mass_old, mass_new):
    owners = mesh.shape["new"]
    olds = mesh.shape["old"]
    n_old, depth = centroids_old.shape
    n_new = centroids_new.shape[0]
    half = n_new // 2
    r = n_new // LANES
    old_steps = olds.bit_length() - 1
    f32 = jnp.float32
    meta_rows = -(-(r + 1) // SUBLANES) * SUBLANES
    left, scales = pl.pallas_call(
        functools.partial(dense_kernel, olds, olds * owners),
        out_shape=(
            pltpu.VMEM((n_old // LANES, LANES), f32),
            pltpu.VMEM((r, LANES), f32),
        ),
        in_specs=[
            pl.BlockSpec(memory_space=pl.ANY),
            pl.BlockSpec(memory_space=pl.ANY),
            pl.BlockSpec(memory_space=pl.ANY),
            pl.BlockSpec(memory_space=pl.ANY),
        ],
        out_specs=(
            pl.BlockSpec(memory_space=pltpu.VMEM),
            pl.BlockSpec(memory_space=pltpu.VMEM),
        ),
        scratch_shapes=[
            pltpu.VMEM((n_old // LANES, LANES), f32),
            pltpu.VMEM((r, LANES), f32),
            pltpu.VMEM((n_old, depth), jnp.bfloat16),
            pltpu.VMEM((owners, 2, half, depth), jnp.bfloat16),
            pltpu.VMEM((2 * owners, n_old, half), f32),
            pltpu.VMEM((n_old, LANES), f32),
            pltpu.VMEM((n_old, LANES), f32),
            pltpu.VMEM((n_old, LANES), f32),
            pltpu.VMEM((n_old, LANES), f32),
            pltpu.VMEM((r, SUBLANES, LANES), f32),
            pltpu.VMEM((owners, r, LANES), f32),
            pltpu.VMEM((owners, r, LANES), f32),
            pltpu.VMEM((meta_rows, LANES), f32),
            pltpu.VMEM((owners - 1, meta_rows, LANES), f32),
            pltpu.VMEM((old_steps + 1, SUBLANES, LANES), f32),
            pltpu.VMEM((old_steps, SUBLANES, LANES), f32),
            pltpu.VMEM((ITERS, owners, r, LANES), f32),
            pltpu.VMEM((ITERS, owners - 1, owners, r, LANES), f32),
            pltpu.SemaphoreType.DMA((5,)),
            pltpu.SemaphoreType.DMA((8,)),
            pltpu.SemaphoreType.DMA((8,)),
            pltpu.SemaphoreType.DMA((owners - 1,)),
            pltpu.SemaphoreType.DMA((owners - 1,)),
            pltpu.SemaphoreType.DMA((old_steps,)),
            pltpu.SemaphoreType.DMA((old_steps,)),
            pltpu.SemaphoreType.DMA((ITERS, owners - 1, owners)),
            pltpu.SemaphoreType.DMA((ITERS, owners - 1, owners)),
        ],
        compiler_params=pltpu.CompilerParams(
            collective_id=0, has_side_effects=True, vmem_limit_bytes=56 * 2**20
        ),
    )(
        centroids_old,
        centroids_new.reshape(2, half, depth),
        mass_old.reshape(n_old // LANES, LANES),
        mass_new.reshape(r, LANES),
    )
    log_old, log_new = pl.pallas_call(
        log_kernel,
        out_shape=(
            jax.ShapeDtypeStruct(left.shape, f32),
            jax.ShapeDtypeStruct(scales.shape, f32),
        ),
        in_specs=[pl.BlockSpec(memory_space=pltpu.VMEM)] * 2,
        out_specs=[pl.BlockSpec(memory_space=pltpu.VMEM)] * 2,
    )(pltpu.with_memory_space_constraint(left, pltpu.VMEM), pltpu.with_memory_space_constraint(scales, pltpu.VMEM))
    return log_old.reshape(-1), log_new.reshape(-1)


def solution(mesh):
    def body(centroids_old, centroids_new, mass_old, mass_new, pairs):
        group_blocks = mesh.shape["new"] * centroids_new.shape[0] // CENTROID_BLOCK
        olds = mesh.shape["old"]
        if group_blocks == PARTNER_BLOCKS and mesh.shape["new"] == 4 and olds & (olds - 1) == 0:
            return dense_body(mesh, centroids_old, centroids_new, mass_old, mass_new)
        return general_body(centroids_old, centroids_new, mass_old, mass_new, pairs)

    return jax.shard_map(
        body,
        mesh=mesh,
        in_specs=(
            P(("old", "new"), None),
            P(("old", "new"), None),
            P(("old", "new")),
            P(("old", "new")),
            P(("old", "new"), None),
        ),
        out_specs=(P(("old", "new")), P(("old", "new"))),
        check_vma=False,
    )
```

```python
import functools
import math

import jax
import jax.numpy as jnp
from jax import lax
from jax.experimental import pallas as pl
from jax.experimental.pallas import tpu as pltpu
from jax.sharding import PartitionSpec as P

D = 768
CENTROID_BLOCK = 256
PARTNER_BLOCKS = 8
ITERS = 3


ENTROPY_SCALE = 0.025


def row_norm_values(blocks):
    return jnp.sqrt(jnp.sum(jnp.square(blocks.astype(jnp.float32)), axis=-1) + 1e-06)


def general_body(centroids_old, centroids_new, mass_old, mass_new, pairs):
    owners = lax.axis_size("new")
    my_old = lax.axis_index("old")
    old_count = centroids_old.shape[0] // CENTROID_BLOCK
    new_count = centroids_new.shape[0] // CENTROID_BLOCK
    devices_all = lax.axis_size("old") * owners
    totals = lax.psum((jnp.sum(mass_old), jnp.sum(mass_new)), ("old", "new"))
    rel_old = (mass_old * (mass_old.shape[0] * devices_all / totals[0])).reshape(
        old_count, CENTROID_BLOCK
    )
    rel_new = (mass_new * (mass_new.shape[0] * devices_all / totals[1])).reshape(
        new_count, CENTROID_BLOCK
    )
    old_blocks = centroids_old.reshape(old_count, CENTROID_BLOCK, D)
    previous_norm = row_norm_values(old_blocks)
    local_ids = pairs - my_old * (owners * new_count)
    everyone = lax.all_gather(centroids_new, "new", axis=0, tiled=True).reshape(
        owners * new_count, CENTROID_BLOCK, D
    )
    norm_all = row_norm_values(everyone)
    chosen = everyone[local_ids]
    selected_norm = norm_all[local_ids]
    columns = owners * new_count
    inner_products = jnp.einsum(
        "rbd,rkcd->rkbc", old_blocks, chosen, preferred_element_type=jnp.float32
    )
    kernel = jnp.exp(
        inner_products
        / (previous_norm[:, None, :, None] * selected_norm[:, :, None, :])
        / ENTROPY_SCALE
    ) * (1.0 / (PARTNER_BLOCKS * CENTROID_BLOCK))
    selector = (local_ids.reshape(-1)[:, None] == jnp.arange(columns)[None, :]).astype(jnp.float32)
    scales = jnp.ones((new_count, CENTROID_BLOCK), jnp.float32)
    left_scale = jnp.ones((old_count, CENTROID_BLOCK), jnp.float32)
    for sweep_index in range(ITERS):
        if sweep_index == 0:
            picked = jnp.ones((old_count, PARTNER_BLOCKS, CENTROID_BLOCK), jnp.float32)
        else:
            fetched = lax.all_gather(scales, "new", axis=0, tiled=True)
            picked = fetched[local_ids]
        row_sum = jnp.einsum("ikbc,ikc->ib", kernel, picked, precision=lax.Precision.HIGHEST)
        left_scale = rel_old / row_sum
        col_terms = jnp.einsum("ikbc,ib->ikc", kernel, left_scale, precision=lax.Precision.HIGHEST)
        gathered_terms = jnp.dot(
            selector.T,
            col_terms.reshape(-1, CENTROID_BLOCK),
            precision=lax.Precision.HIGHEST,
            preferred_element_type=jnp.float32,
        )
        column = lax.psum_scatter(gathered_terms, "new", scatter_dimension=0, tiled=True)
        scales = rel_new / column
    return (jnp.log(left_scale).reshape(-1), jnp.log(scales).reshape(-1))


MESH = pl.DeviceIdType.MESH
LANES = 128
SUBLANES = 8
TILE = 256
STAGE_TILE = 512
UNROLL = 4


def eye_mask():
    shape = (LANES, LANES)
    return lax.broadcasted_iota(jnp.int32, shape, 0) == lax.broadcasted_iota(jnp.int32, shape, 1)


def to_row(column, eye):
    wide = jnp.broadcast_to(column, (LANES, LANES))
    return jnp.sum(jnp.where(eye, wide, 0.0), axis=0, keepdims=True)


def to_column(row, eye):
    wide = jnp.broadcast_to(row, (LANES, LANES))
    return jnp.sum(jnp.where(eye, wide, 0.0), axis=1, keepdims=True)


def dense_kernel(
    olds,
    devices_all,
    old_hbm,
    new_hbm,
    mass_old_hbm,
    mass_new_hbm,
    left_ref,
    scales_ref,
    mass_old_ref,
    mass_new_ref,
    a_ref,
    b_ref,
    k_ref,
    inv_old,
    mass_wide,
    row_acc,
    u_ref,
    col_acc,
    v_ref,
    rel_new,
    meta,
    meta_in,
    sums,
    sums_in,
    cols,
    cols_in,
    load_sem,
    gather_send,
    gather_recv,
    meta_send,
    meta_recv,
    sums_send,
    sums_recv,
    cols_send,
    cols_recv,
):
    me = lax.axis_index("new")
    my_old = lax.axis_index("old")
    flip_x = 1 - 2 * lax.rem(me, 2)
    flip_y = 2 - 4 * lax.div(me, 2)
    peers = (None, me + flip_x, me + flip_y, me + flip_x + flip_y)
    chips = olds // 2
    core, chip = lax.rem(my_old, 2), lax.div(my_old, 2)
    partner = my_old + 1 - 2 * core

    n_old = a_ref.shape[0]
    half = b_ref.shape[2]
    depth = a_ref.shape[1]
    r = mass_new_ref.shape[0]
    tiles = n_old // TILE
    per_tile = TILE // LANES
    per_half = half // LANES
    scale = float(PARTNER_BLOCKS * CENTROID_BLOCK)
    eye = eye_mask()

    load_a = pltpu.make_async_copy(old_hbm, a_ref, load_sem.at[0])
    load_b = [
        pltpu.make_async_copy(new_hbm.at[h], b_ref.at[0, h], load_sem.at[1 + h]) for h in range(2)
    ]
    load_mass = [
        pltpu.make_async_copy(mass_old_hbm, mass_old_ref, load_sem.at[3]),
        pltpu.make_async_copy(mass_new_hbm, mass_new_ref, load_sem.at[4]),
    ]
    barrier = pltpu.get_barrier_semaphore()
    for p in range(1, 4):
        pl.semaphore_signal(barrier, inc=1, device_id={"new": peers[p]}, device_id_type=MESH)
    pl.semaphore_signal(barrier, inc=1, device_id={"old": partner}, device_id_type=MESH)

    @pl.when(chip > 0)
    def _():
        pl.semaphore_signal(barrier, inc=1, device_id={"old": my_old - 2}, device_id_type=MESH)

    @pl.when(chip < chips - 1)
    def _():
        pl.semaphore_signal(barrier, inc=1, device_id={"old": my_old + 2}, device_id_type=MESH)

    for copy in load_mass + [load_a] + load_b:
        copy.start()
    ends = lax.convert_element_type(chip > 0, jnp.int32)
    ends = ends + lax.convert_element_type(chip < chips - 1, jnp.int32)
    pl.semaphore_wait(barrier, 4 + ends)

    meta_copies = [
        pltpu.make_async_remote_copy(
            src_ref=meta,
            dst_ref=meta_in.at[p - 1],
            send_sem=meta_send.at[p - 1],
            recv_sem=meta_recv.at[p - 1],
            device_id={"new": peers[p]},
            device_id_type=MESH,
        )
        for p in range(1, 4)
    ]

    def send(index, src, slot, h, p, part=None):
        return pltpu.make_async_remote_copy(
            src_ref=src,
            dst_ref=b_ref.at[slot, h] if part is None else b_ref.at[slot, h, part],
            send_sem=gather_send.at[index],
            recv_sem=gather_recv.at[index],
            device_id={"new": peers[p]},
            device_id_type=MESH,
        )

    moves = [
        send(0, new_hbm.at[1], 1, 1, 1),
        send(1, new_hbm.at[0], 1, 0, 1),
        send(2, new_hbm.at[0], 2, 0, 2),
        send(3, new_hbm.at[1], 2, 1, 2),
    ]
    quarters = [pl.ds(q * (half // 2), half // 2) for q in range(2)]
    relay_x = [send(4 + q, b_ref.at[2, 0, quarters[q]], 3, 0, 1, quarters[q]) for q in range(2)]
    relay_y = [send(6 + q, b_ref.at[1, 1, quarters[q]], 3, 1, 2, quarters[q]) for q in range(2)]

    def start(copies):
        def begin():
            for copy in copies:
                copy.start()

        return begin

    for copy in load_mass:
        copy.wait()
    meta[...] = jnp.zeros_like(meta)
    meta[0:r, :] = mass_new_ref[...]
    meta[r : r + 1, :] = jnp.sum(mass_old_ref[...], axis=0, keepdims=True)
    for copy in meta_copies:
        copy.start()
    start([moves[0], moves[2]])()
    pl.when(core == 0)(start([moves[1], moves[3]]))
    load_a.wait()

    @pl.loop(0, tiles)
    def _(t):
        rows = pl.ds(pl.multiple_of(t * TILE, TILE), TILE)
        a = a_ref[rows, :].astype(jnp.float32)
        total = jnp.sum(a * a, axis=1, keepdims=True)
        inv_old[rows, :] = jnp.broadcast_to(1.0 / jnp.sqrt(total + 1e-06), (TILE, LANES))
        for i in range(per_tile):
            part = pl.ds(pl.multiple_of(t * TILE + i * LANES, LANES), LANES)
            column = to_column(mass_old_ref[pl.ds(t * per_tile + i, 1), :], eye)
            mass_wide[part, :] = jnp.broadcast_to(column * scale, (LANES, LANES))

    def stage(chunks, first, start=0, width=None):
        width = half if width is None else width
        factors = []
        for slot, h in chunks:
            b = b_ref[slot, h, start : start + width].astype(jnp.float32)
            total = jnp.sum(b * b, axis=1, keepdims=True)
            inverse = (math.log2(math.e) / ENTROPY_SCALE) / jnp.sqrt(total + 1e-06)
            factors.append(
                [to_row(inverse[j : j + LANES], eye) for j in range(0, width, LANES)]
            )

        @pl.loop(0, n_old // STAGE_TILE)
        def _(t):
            rows = pl.ds(pl.multiple_of(t * STAGE_TILE, STAGE_TILE), STAGE_TILE)
            a = a_ref[rows, :]
            inv = inv_old[rows, :]
            acc = jnp.zeros((STAGE_TILE, LANES), jnp.float32) if first else row_acc[rows, :]
            for some in [chunks] if width < half else [(chunk,) for chunk in chunks]:
                blocks = [b_ref[slot, h, start : start + width] for slot, h in some]
                products = lax.dot_general(
                    a,
                    jnp.concatenate(blocks, axis=0) if len(blocks) > 1 else blocks[0],
                    (((1,), (1,)), ((), ())),
                    preferred_element_type=jnp.float32,
                )
                for i, (slot, h) in enumerate(some):
                    factor = factors[chunks.index((slot, h))]
                    for j in range(0, width, LANES):
                        part = products[:, i * width + j : i * width + j + LANES]
                        k = jnp.exp2(part * inv * factor[j // LANES])
                        k_ref[2 * slot + h, rows, start + j : start + j + LANES] = k
                        acc = acc + k
            row_acc[rows, :] = acc

    for copy in load_b:
        copy.wait()
    pair_copy = pltpu.make_async_remote_copy(
        src_ref=sums.at[0],
        dst_ref=sums.at[1],
        send_sem=sums_send.at[0],
        recv_sem=sums_recv.at[0],
        device_id={"old": partner},
        device_id_type=MESH,
    )

    def flood_copy(side, k):
        index = 1 + 2 * k + side
        return pltpu.make_async_remote_copy(
            src_ref=sums.at[2] if k == 0 else sums_in.at[side, k - 1],
            dst_ref=sums_in.at[side, k],
            send_sem=sums_send.at[index],
            recv_sem=sums_recv.at[index],
            device_id={"old": my_old + 2 - 4 * side},
            device_id_type=MESH,
        )

    def sends(side, k):
        here = chip if side == 0 else chips - 1 - chip
        return jnp.logical_and(here < chips - 1, here >= k)

    def receives(side, k):
        here = chip if side == 0 else chips - 1 - chip
        return here > k

    def advance(step):
        if step == 0:
            for copy in meta_copies:
                copy.wait()
            old_sum = meta[r : r + 1, :]
            new_sum = jnp.sum(meta[0:r, :], axis=0, keepdims=True)
            for p in range(1, 4):
                old_sum = old_sum + meta_in[p - 1, r : r + 1, :]
                new_sum = new_sum + jnp.sum(meta_in[p - 1, 0:r, :], axis=0, keepdims=True)
            sums[0] = jnp.zeros((SUBLANES, LANES), jnp.float32)
            sums[0, 0:1, :] = old_sum
            sums[0, 1:2, :] = new_sum
            pair_copy.start()
        elif step == 1:
            pair_copy.wait()
            sums[2] = sums[0] + sums[1]
            sums[3] = sums[2]
        if 1 < step <= chips:
            for side in range(2):

                @pl.when(receives(side, step - 2))
                def _():
                    flood_copy(side, step - 2).wait_recv()
                    sums[3] = sums[3] + sums_in[side, step - 2]

        if 1 <= step < chips:
            for side in range(2):
                pl.when(sends(side, step - 1))(flood_copy(side, step - 1).start)

    def finish_floods():
        for k in range(chips - 1):
            for side in range(2):
                pl.when(sends(side, k))(flood_copy(side, k).wait_send)

    stage(((0, 0), (0, 1)), True)
    advance(0)
    moves[0].wait_recv()
    pl.when(core == 0)(start(relay_y))
    moves[2].wait_recv()
    pl.when(core == 0)(start(relay_x))
    stage(((1, 1), (2, 0)), False)
    pl.when(core == 1)(start([moves[1], moves[3]] + relay_y + relay_x))
    advance(1)
    moves[1].wait_recv()
    moves[3].wait_recv()
    stage(((1, 0), (2, 1)), False)
    advance(2)
    rel_new[0] = meta[0:r, :] * scale
    for p in range(1, 4):
        rel_new[p] = meta_in[p - 1, 0:r, :] * scale
    for piece in range(2):
        relay_x[piece].wait_recv()
        relay_y[piece].wait_recv()
        stage(((3, 0), (3, 1)), False, piece * (half // 2), half // 2)
    for move in moves + relay_x + relay_y:
        move.wait_send()

    my_x, my_y = lax.rem(me, 2), lax.div(me, 2)

    def slot_of(owner):
        x = 1 - my_x if owner % 2 else my_x
        y = 1 - my_y if owner // 2 else my_y
        return x + 2 * y

    def col_sums(slot):
        @pl.loop(0, tiles // UNROLL, init_carry=[jnp.zeros((SUBLANES, LANES), jnp.float32)] * r)
        def sums_of(t, carry):
            for b in range(UNROLL):
                start = (t * UNROLL + b) * TILE
                rows = pl.ds(pl.multiple_of(start, TILE), TILE)
                u = u_ref[rows, :]
                new = []
                for g in range(r):
                    c, j = 2 * slot + g // per_half, g % per_half
                    part = k_ref[c, rows, j * LANES : (j + 1) * LANES] * u
                    part = part.reshape(TILE // SUBLANES, SUBLANES, LANES)
                    new.append(carry[g] + jnp.sum(part, axis=0))
                carry = new
            return carry

        for g in range(r):
            col_acc[g] = sums_of[g]
        return jnp.sum(col_acc[...], axis=1)

    def add_rows(slot, owner, first):
        @pl.loop(0, tiles // UNROLL)
        def _(t):
            for b in range(UNROLL):
                start = (t * UNROLL + b) * TILE
                rows = pl.ds(pl.multiple_of(start, TILE), TILE)
                acc = jnp.zeros((TILE, LANES), jnp.float32) if first else row_acc[rows, :]
                for g in range(r):
                    c, j = 2 * slot + g // per_half, g % per_half
                    weights = v_ref[owner, g : g + 1, :]
                    acc = acc + k_ref[c, rows, j * LANES : (j + 1) * LANES] * weights
                row_acc[rows, :] = acc

    def exchange(sweep, index, p, src):
        return pltpu.make_async_remote_copy(
            src_ref=cols.at[sweep, src],
            dst_ref=cols_in.at[sweep, p - 1, index],
            send_sem=cols_send.at[sweep, p - 1, index],
            recv_sem=cols_recv.at[sweep, p - 1, index],
            device_id={"new": peers[p]},
            device_id_type=MESH,
        )

    for sweep in range(ITERS):
        last = sweep == ITERS - 1

        @pl.loop(0, n_old // STAGE_TILE)
        def _(t):
            rows = pl.ds(pl.multiple_of(t * STAGE_TILE, STAGE_TILE), STAGE_TILE)
            row_sum = jnp.sum(row_acc[rows, :], axis=1, keepdims=True)
            u_ref[rows, :] = mass_wide[rows, :] / jnp.broadcast_to(row_sum, (STAGE_TILE, LANES))

        if last:
            copies = []
            for p in (3, 2, 1):
                cols[sweep, p] = col_sums(p)
                copies.append(exchange(sweep, 0, p, p))
                copies[-1].start()
            total = col_sums(0)
            for step in range(ITERS + 2, chips + 1):
                advance(step)
            finish_floods()
            totals = jnp.sum(sums[3], axis=1, keepdims=True)
            alpha = n_old * devices_all / totals[0:1, :]
            beta = r * LANES * devices_all / totals[1:2, :]
            ratio = alpha / beta
            left_factor, scales_factor = alpha, 1.0 / ratio
            for _ in range(ITERS - 1):
                left_factor, scales_factor = left_factor * ratio, scales_factor / ratio
            for i in range(n_old // LANES):
                left_ref[i : i + 1, :] = (
                    to_row(u_ref[i * LANES : (i + 1) * LANES, :], eye) * left_factor
                )
            for copy in copies:
                copy.wait()
            for p in range(1, 4):
                total = total + cols_in[sweep, p - 1, 0]
            scales_ref[...] = rel_new[0] / total * scales_factor
        else:
            copies = []
            for owner in range(4):
                cols[sweep, owner] = col_sums(slot_of(owner))
                copies.append([exchange(sweep, owner, p, owner) for p in (3, 2, 1)])
                for copy in copies[-1]:
                    copy.start()
            advance(3 + sweep)
            for owner in range(4):
                for copy in copies[owner]:
                    copy.wait()
                slot = slot_of(owner)
                total = cols[sweep, owner]
                for p in range(1, 4):
                    total = total + cols_in[sweep, p - 1, owner]
                v_ref[owner] = rel_new[slot] / total
                add_rows(slot, owner, owner == 0)


def log_kernel(left_ref, scales_ref, log_old_ref, log_new_ref):
    log_old_ref[...] = jnp.log(left_ref[...])
    log_new_ref[...] = jnp.log(scales_ref[...])


def dense_body(mesh, centroids_old, centroids_new, mass_old, mass_new):
    owners = mesh.shape["new"]
    olds = mesh.shape["old"]
    n_old, depth = centroids_old.shape
    n_new = centroids_new.shape[0]
    half = n_new // 2
    r = n_new // LANES
    chips = olds // 2
    f32 = jnp.float32
    meta_rows = -(-(r + 1) // SUBLANES) * SUBLANES
    left, scales = pl.pallas_call(
        functools.partial(dense_kernel, olds, olds * owners),
        out_shape=(
            pltpu.VMEM((n_old // LANES, LANES), f32),
            pltpu.VMEM((r, LANES), f32),
        ),
        in_specs=[
            pl.BlockSpec(memory_space=pl.ANY),
            pl.BlockSpec(memory_space=pl.ANY),
            pl.BlockSpec(memory_space=pl.ANY),
            pl.BlockSpec(memory_space=pl.ANY),
        ],
        out_specs=(
            pl.BlockSpec(memory_space=pltpu.VMEM),
            pl.BlockSpec(memory_space=pltpu.VMEM),
        ),
        scratch_shapes=[
            pltpu.VMEM((n_old // LANES, LANES), f32),
            pltpu.VMEM((r, LANES), f32),
            pltpu.VMEM((n_old, depth), jnp.bfloat16),
            pltpu.VMEM((owners, 2, half, depth), jnp.bfloat16),
            pltpu.VMEM((2 * owners, n_old, half), f32),
            pltpu.VMEM((n_old, LANES), f32),
            pltpu.VMEM((n_old, LANES), f32),
            pltpu.VMEM((n_old, LANES), f32),
            pltpu.VMEM((n_old, LANES), f32),
            pltpu.VMEM((r, SUBLANES, LANES), f32),
            pltpu.VMEM((owners, r, LANES), f32),
            pltpu.VMEM((owners, r, LANES), f32),
            pltpu.VMEM((meta_rows, LANES), f32),
            pltpu.VMEM((owners - 1, meta_rows, LANES), f32),
            pltpu.VMEM((4, SUBLANES, LANES), f32),
            pltpu.VMEM((2, max(chips - 1, 1), SUBLANES, LANES), f32),
            pltpu.VMEM((ITERS, owners, r, LANES), f32),
            pltpu.VMEM((ITERS, owners - 1, owners, r, LANES), f32),
            pltpu.SemaphoreType.DMA((5,)),
            pltpu.SemaphoreType.DMA((8,)),
            pltpu.SemaphoreType.DMA((8,)),
            pltpu.SemaphoreType.DMA((owners - 1,)),
            pltpu.SemaphoreType.DMA((owners - 1,)),
            pltpu.SemaphoreType.DMA((2 * chips + 1,)),
            pltpu.SemaphoreType.DMA((2 * chips + 1,)),
            pltpu.SemaphoreType.DMA((ITERS, owners - 1, owners)),
            pltpu.SemaphoreType.DMA((ITERS, owners - 1, owners)),
        ],
        compiler_params=pltpu.CompilerParams(
            collective_id=0, has_side_effects=True, vmem_limit_bytes=56 * 2**20
        ),
    )(
        centroids_old,
        centroids_new.reshape(2, half, depth),
        mass_old.reshape(n_old // LANES, LANES),
        mass_new.reshape(r, LANES),
    )
    log_old, log_new = pl.pallas_call(
        log_kernel,
        out_shape=(
            jax.ShapeDtypeStruct(left.shape, f32),
            jax.ShapeDtypeStruct(scales.shape, f32),
        ),
        in_specs=[pl.BlockSpec(memory_space=pltpu.VMEM)] * 2,
        out_specs=[pl.BlockSpec(memory_space=pltpu.VMEM)] * 2,
    )(pltpu.with_memory_space_constraint(left, pltpu.VMEM), pltpu.with_memory_space_constraint(scales, pltpu.VMEM))
    return log_old.reshape(-1), log_new.reshape(-1)


def solution(mesh):
    def body(centroids_old, centroids_new, mass_old, mass_new, pairs):
        group_blocks = mesh.shape["new"] * centroids_new.shape[0] // CENTROID_BLOCK
        olds = mesh.shape["old"]
        if group_blocks == PARTNER_BLOCKS and mesh.shape["new"] == 4 and olds % 2 == 0:
            return dense_body(mesh, centroids_old, centroids_new, mass_old, mass_new)
        return general_body(centroids_old, centroids_new, mass_old, mass_new, pairs)

    return jax.shard_map(
        body,
        mesh=mesh,
        in_specs=(
            P(("old", "new"), None),
            P(("old", "new"), None),
            P(("old", "new")),
            P(("old", "new")),
            P(("old", "new"), None),
        ),
        out_specs=(P(("old", "new")), P(("old", "new"))),
        check_vma=False,
    )
```
